512 devices in a mesh: lat: 8 (over y_lo, x), lon: 64 (over z, y_hi, core).
Axes of the slice: x: 4, y: 4 (y_hi: 2, y_lo: 2; y = y_hi * 2 + y_lo), z: 16, core: 2. Of those that a mesh axis runs over, the one named last changes fastest.
Arguments:
- heights: bfloat16 [4, 2048, 32768], P(None, 'lat', 'lon'), may hold values from -24 to 24
- sigma_class: int32 [2048, 32768], P('lat', 'lon'), may hold values from 0 to 15
- window_class: int32 [2048, 32768], P('lat', 'lon'), may hold values from 0 to 15
- sigma_table: float32 [16], replicated, may hold values from 0.3 to 32, as said below
- window_table: float32 [16], replicated, may hold values from 0.3 to 32, as said below
Outputs:
- smoothed: bfloat16 [4, 2048, 32768], P(None, 'lat', 'lon')
The draws below stay inside these ranges and needn't reach their ends.
Inputs may be any that keep to these rules, and one draw needn't show every extreme that they name: `sigma_table`: widths of the first smoothing's classes, in cells. `window_table`: widths of the second smoothing's classes, in cells.
All inputs are finite; a program needn't handle non-finite values.
Results may differ from the reference program's by a relative error of at most 0.0046.
Values may be sent and summed in bfloat16 or wider, within the bound.
No kernel may reach another device: no remote copies, remote signals or barrier semaphores. Data moves between devices by JAX's collectives and lax.ppermute only.
A program may use at most 64 MiB of HBM per device.

```python
import math
import jax
import jax.numpy as jnp
from jax import lax

BANDS = 4
RADIUS = 16
NCLASS = 16
NLAT = 2048
NLON = 32768


narrowest = 0.3


broadest = 32.0


def table_draw(key, salt):
    base = jax.random.fold_in(key, salt)
    order = jax.random.permutation(jax.random.fold_in(base, 1), NCLASS).astype(jnp.float32)
    jitter = jax.random.uniform(jax.random.fold_in(base, 2), (NCLASS,), jnp.float32)
    position = (order + jitter) / float(NCLASS)
    widths = narrowest * jnp.exp(position * math.log(broadest / narrowest))
    return jnp.clip(widths, narrowest, broadest).astype(jnp.float32)


def draw_sigma_table(key, part):
    return table_draw(key, 101)


def draw_window_table(key, part):
    return table_draw(key, 202)


def with_ends(values, key, low, largest):
    longest = values.shape.index(max(values.shape))
    spots = []
    for shift in (0, 1):
        where = [jax.random.randint(jax.random.fold_in(key, axis), (), 0, length) for axis, length in enumerate(values.shape)]
        where[longest] = (where[longest] + shift) % values.shape[longest]
        spots.append(tuple(where))
    return values.at[spots[0]].set(low).at[spots[1]].set(largest)


def shard_levels(key, extent, split, smallest, largest):
    gain = 1.0
    for dim, shards_of in split:
        steps = jax.random.uniform(jax.random.fold_in(jax.random.fold_in(key, 6), dim), (shards_of,), jnp.float32, smallest / len(split), largest / len(split))
        gain = gain * jnp.repeat(jnp.exp(steps), extent[dim] // shards_of).reshape((-1,) + (1,) * (len(extent) - 1 - dim))
    return gain


def normal_values(stream_key, dims, width, limit, pieces=(), kind=jnp.bfloat16):
    array = width * jax.random.normal(stream_key, dims, jnp.float32)
    if pieces:
        array = array * shard_levels(stream_key, dims, pieces, -0.22, 0.18)
    return jnp.clip(array, -limit, limit).astype(kind)


def setup_inputs(seed: int = 0) -> dict:
    arg_keys = jax.random.split(jax.random.key(seed), 6)
    heights = normal_values(arg_keys[0], (BANDS, NLAT, NLON), 4.0, 24.0, ((1, 8), (2, 64)))
    sigma_class = with_ends(jax.random.randint(arg_keys[1], (NLAT, NLON), 0, NCLASS), jax.random.fold_in(arg_keys[1], 1), 0, NCLASS - 1).astype(jnp.int32)
    window_class = with_ends(jax.random.randint(arg_keys[2], (NLAT, NLON), 0, NCLASS), jax.random.fold_in(arg_keys[2], 1), 0, NCLASS - 1).astype(jnp.int32)
    sigma_table = draw_sigma_table(jax.random.fold_in(arg_keys[5], 71), 0)
    window_table = draw_window_table(jax.random.fold_in(arg_keys[5], 71), 0)
    return {"heights": heights, "sigma_class": sigma_class, "window_class": window_class, "sigma_table": sigma_table, "window_table": window_table}


def class_weights(classes, table):
    spread_tab = 0.5 / (table * table)
    offsets = jnp.arange(-RADIUS, RADIUS + 1).astype(jnp.float32)
    norm = jnp.sum(jnp.exp(-(offsets * offsets)[None, :] * spread_tab[:, None]), axis=1)
    scale_tab = 1.0 / norm
    spread = jnp.zeros(classes.shape, jnp.float32)
    scale_cell = jnp.zeros(classes.shape, jnp.float32)
    for number in range(NCLASS):
        hit = classes == number
        spread = jnp.where(hit, spread_tab[number], spread)
        scale_cell = jnp.where(hit, scale_tab[number], scale_cell)
    return spread, scale_cell


def smooth(field, classes, table):
    spread, scale_cell = class_weights(classes, table)

    def one_band(plane):
        padded = jnp.pad(plane.astype(jnp.float32), ((RADIUS, RADIUS), (0, 0)))
        accum = jnp.zeros(spread.shape, jnp.float32)
        for offset in range(-RADIUS, RADIUS + 1):
            weight = jnp.exp(-float(offset * offset) * spread)
            accum = accum + weight * padded[RADIUS + offset:RADIUS + offset + NLAT, :]
        upper = accum * scale_cell
        widened = jnp.pad(upper, ((0, 0), (RADIUS, RADIUS)))
        total = jnp.zeros(spread.shape, jnp.float32)
        for offset in range(-RADIUS, RADIUS + 1):
            weight = jnp.exp(-float(offset * offset) * spread)
            total = total + weight * widened[:, RADIUS + offset:RADIUS + offset + NLON]
        return (total * scale_cell).astype(jnp.bfloat16)

    return lax.map(one_band, field)


def reference(heights, sigma_class, window_class, sigma_table, window_table):
    first = smooth(heights, sigma_class, sigma_table)
    return smooth(first, window_class, window_table)
```

```python
import jax
import jax.numpy as jnp
from jax import lax
from jax.experimental import pallas as pl
from jax.experimental.pallas import tpu as pltpu
from jax.sharding import PartitionSpec as P

RADIUS = 16
NCLASS = 16
BANDS = 4
ROWS = 256
COLS = 512
LANES = 128
COLBLK = COLS // LANES
ROWBLK = ROWS // LANES
WIDE = 2 * RADIUS
TALL = ROWS + 2 * RADIUS
FULL = ROWS + 2 * WIDE
BROAD = COLS + 2 * RADIUS
CODES = TALL // 2


def lookup(table, codes):
    return jnp.take_along_axis(jnp.broadcast_to(table, codes.shape), codes, axis=1)


def weighted(sources, q, scale):
    square = q * q
    weight = q
    ratio = q * square
    totals = [source(0) for source in sources]
    for k in range(1, RADIUS + 1):
        if k > 1:
            weight = weight * ratio
            ratio = ratio * square
        totals = [
            total + weight * (source(k) + source(-k)) for total, source in zip(totals, sources)
        ]
    return [total * scale for total in totals]


def smooth_blocks(source_ref, blocks, lead, code_ref, code_block, q_tab, s_tab, out_ref, length, rounded=False):
    def tile(step, _):
        start = pl.multiple_of(step * 8, 8)
        codes = code_ref[code_block, pl.ds(start, 8), :]
        q = lookup(q_tab, codes)
        scale = lookup(s_tab, codes)

        def reader(block):
            return lambda k: source_ref[block, pl.ds(start + lead + k, 8), :]

        results = weighted([reader(block) for block in blocks], q, scale)
        for block, result in zip(blocks, results):
            if rounded:
                result = result.astype(jnp.bfloat16).astype(jnp.float32)
            out_ref[block, pl.ds(start, 8), :] = result
        return 0

    lax.fori_loop(0, length // 8, tile, 0, unroll=2)


def kernel(
    tables_ref, heights_ref, low_ref, high_ref, left_ref, right_ref, sigma_ref, window_ref, out_ref,
    rows_in, rows_out, cols_in, cols_out, sig_row, sig_col, win_row, win_col,
):
    q_sig = tables_ref[0:1, :]
    s_sig = tables_ref[1:2, :]
    q_win = tables_ref[2:3, :]
    s_win = tables_ref[3:4, :]

    for b in range(BANDS):
        for j in range(COLBLK):
            lanes = slice(j * LANES, (j + 1) * LANES)
            block = b * COLBLK + j
            rows_in[block, 0:WIDE, :] = low_ref[b * WIDE:(b + 1) * WIDE, lanes].astype(jnp.float32)
            rows_in[block, WIDE:WIDE + ROWS, :] = heights_ref[b, :, lanes].astype(jnp.float32)
            rows_in[block, WIDE + ROWS:FULL, :] = high_ref[b * WIDE:(b + 1) * WIDE, lanes].astype(jnp.float32)
    rows_in[16, :, :] = left_ref[0:FULL, :].astype(jnp.float32)
    rows_in[17, :, :] = right_ref[0:FULL, :].astype(jnp.float32)

    for j in range(COLBLK):
        lanes = slice(j * LANES, (j + 1) * LANES)
        edge = slice(BANDS * WIDE, BANDS * WIDE + RADIUS)
        sig_row[j, 0:RADIUS, :] = low_ref[edge, lanes].astype(jnp.float32).astype(jnp.int32)
        sig_row[j, RADIUS:RADIUS + ROWS, :] = sigma_ref[:, lanes] + 1
        sig_row[j, RADIUS + ROWS:TALL, :] = high_ref[edge, lanes].astype(jnp.float32).astype(jnp.int32)
        win_row[j, :, :] = window_ref[:, lanes] + 1
    halves = []
    for side, ref in ((4, left_ref), (5, right_ref)):
        packed = ref[FULL:FULL + CODES, :].astype(jnp.float32).astype(jnp.int32)
        for half in range(2):
            piece = packed[:, half * WIDE:(half + 1) * WIDE]
            sig_row[side, half * CODES:(half + 1) * CODES, :] = jnp.concatenate([piece] * BANDS, axis=1)
        halves.append([packed[0:LANES, 2 * WIDE + h * RADIUS:2 * WIDE + (h + 1) * RADIUS] for h in range(2)])
    for half in range(2):
        pair = [halves[0][half], halves[1][half]]
        win_row[4, half * LANES:(half + 1) * LANES, :] = jnp.concatenate(pair * BANDS, axis=1)

    for j in range(COLBLK):
        for i in range(ROWBLK):
            body = sig_row[j, RADIUS + i * LANES:RADIUS + (i + 1) * LANES, :]
            sig_col[i, RADIUS + j * LANES:RADIUS + (j + 1) * LANES, :] = body.T
            win_col[i, j * LANES:(j + 1) * LANES, :] = win_row[j, i * LANES:(i + 1) * LANES, :].T
        edges = jnp.concatenate([sig_row[j, 0:RADIUS, :], sig_row[j, RADIUS + ROWS:TALL, :]] * BANDS, axis=0)
        sig_col[2, RADIUS + j * LANES:RADIUS + (j + 1) * LANES, :] = edges.T
    for side, block in enumerate((4, 5)):
        inner = slice(RADIUS, WIDE) if side == 0 else slice(0, RADIUS)
        place = slice(0, RADIUS) if side == 0 else slice(RADIUS + COLS, BROAD)
        for i in range(ROWBLK):
            body = sig_row[block, RADIUS + i * LANES:RADIUS + (i + 1) * LANES, :].T
            sig_col[i, place, :] = body[inner, :]
        edges = jnp.concatenate([sig_row[block, 0:RADIUS, :], sig_row[block, RADIUS + ROWS:TALL, :]] * BANDS, axis=0)
        sig_col[2, place, :] = edges.T[inner, :]

    for j in range(COLBLK):
        blocks = [b * COLBLK + j for b in range(BANDS)]
        smooth_blocks(rows_in, blocks, RADIUS, sig_row, j, q_sig, s_sig, rows_out, TALL)
    for side in range(2):
        smooth_blocks(rows_in, [16 + side], RADIUS, sig_row, 4 + side, q_sig, s_sig, rows_out, TALL)

    for j in range(COLBLK):
        place = slice(WIDE + j * LANES, WIDE + (j + 1) * LANES)
        for b in range(BANDS):
            for i in range(ROWBLK):
                body = rows_out[b * COLBLK + j, RADIUS + i * LANES:RADIUS + (i + 1) * LANES, :]
                cols_in[b * ROWBLK + i, place, :] = body.T
        edges = []
        for b in range(BANDS):
            edges += [rows_out[b * COLBLK + j, 0:RADIUS, :], rows_out[b * COLBLK + j, RADIUS + ROWS:TALL, :]]
        cols_in[8, place, :] = jnp.concatenate(edges, axis=0).T
    for side in range(2):
        place = slice(0, WIDE) if side == 0 else slice(WIDE + COLS, 2 * WIDE + COLS)
        for i in range(ROWBLK):
            body = rows_out[16 + side, RADIUS + i * LANES:RADIUS + (i + 1) * LANES, :].T
            for b in range(BANDS):
                cols_in[b * ROWBLK + i, place, :] = body[b * WIDE:(b + 1) * WIDE, :]
        top = rows_out[16 + side, 0:RADIUS, :]
        bottom = rows_out[16 + side, RADIUS + ROWS:TALL, :]
        edges = jnp.concatenate([top, bottom] * BANDS, axis=0).T
        lane = lax.broadcasted_iota(jnp.int32, (WIDE, LANES), 1) // WIDE
        merged = edges[0:WIDE, :]
        for b in range(1, BANDS):
            merged = jnp.where(lane == b, edges[b * WIDE:(b + 1) * WIDE, :], merged)
        cols_in[8, place, :] = merged

    for i in range(ROWBLK):
        blocks = [b * ROWBLK + i for b in range(BANDS)]
        smooth_blocks(cols_in, blocks, RADIUS, sig_col, i, q_sig, s_sig, cols_out, BROAD, True)
    smooth_blocks(cols_in, [8], RADIUS, sig_col, 2, q_sig, s_sig, cols_out, BROAD, True)

    for j in range(COLBLK):
        place = slice(RADIUS + j * LANES, RADIUS + (j + 1) * LANES)
        for b in range(BANDS):
            for i in range(ROWBLK):
                rows_in[b * COLBLK + j, RADIUS + i * LANES:RADIUS + (i + 1) * LANES, :] = cols_out[b * ROWBLK + i, place, :].T
        edges = cols_out[8, place, :].T
        for b in range(BANDS):
            rows_in[b * COLBLK + j, 0:RADIUS, :] = edges[b * WIDE:b * WIDE + RADIUS, :]
            rows_in[b * COLBLK + j, RADIUS + ROWS:TALL, :] = edges[b * WIDE + RADIUS:(b + 1) * WIDE, :]
    for i in range(ROWBLK):
        edges = []
        for b in range(BANDS):
            edges += [cols_out[b * ROWBLK + i, 0:RADIUS, :], cols_out[b * ROWBLK + i, RADIUS + COLS:BROAD, :]]
        rows_in[16, RADIUS + i * LANES:RADIUS + (i + 1) * LANES, :] = jnp.concatenate(edges, axis=0).T
    both = jnp.concatenate([cols_out[8, 0:RADIUS, :], cols_out[8, RADIUS + COLS:BROAD, :]] * BANDS, axis=0).T
    lane = lax.broadcasted_iota(jnp.int32, (WIDE, LANES), 1) // WIDE
    merged = both[0:WIDE, :]
    for b in range(1, BANDS):
        merged = jnp.where(lane == b, both[b * WIDE:(b + 1) * WIDE, :], merged)
    rows_in[16, 0:RADIUS, :] = merged[0:RADIUS, :]
    rows_in[16, RADIUS + ROWS:TALL, :] = merged[RADIUS:WIDE, :]

    for j in range(COLBLK):
        blocks = [b * COLBLK + j for b in range(BANDS)]
        smooth_blocks(rows_in, blocks, RADIUS, win_row, j, q_win, s_win, rows_out, ROWS)
    smooth_blocks(rows_in, [16], RADIUS, win_row, 4, q_win, s_win, rows_out, ROWS)

    for i in range(ROWBLK):
        for j in range(COLBLK):
            for b in range(BANDS):
                body = rows_out[b * COLBLK + j, i * LANES:(i + 1) * LANES, :]
                cols_in[b * ROWBLK + i, RADIUS + j * LANES:RADIUS + (j + 1) * LANES, :] = body.T
        body = rows_out[16, i * LANES:(i + 1) * LANES, :].T
        for b in range(BANDS):
            cols_in[b * ROWBLK + i, 0:RADIUS, :] = body[b * WIDE:b * WIDE + RADIUS, :]
            cols_in[b * ROWBLK + i, RADIUS + COLS:BROAD, :] = body[b * WIDE + RADIUS:(b + 1) * WIDE, :]

    for i in range(ROWBLK):
        blocks = [b * ROWBLK + i for b in range(BANDS)]
        smooth_blocks(cols_in, blocks, RADIUS, win_col, i, q_win, s_win, cols_out, COLS)

    for b in range(BANDS):
        for i in range(ROWBLK):
            for j in range(COLBLK):
                body = cols_out[b * ROWBLK + i, j * LANES:(j + 1) * LANES, :].T
                out_ref[b, i * LANES:(i + 1) * LANES, j * LANES:(j + 1) * LANES] = body.astype(jnp.bfloat16)


def class_tables(table):
    spread = 0.5 / (table * table)
    offsets = jnp.arange(-RADIUS, RADIUS + 1).astype(jnp.float32)
    norm = jnp.sum(jnp.exp(-(offsets * offsets)[None, :] * spread[:, None]), axis=1)
    return jnp.pad(jnp.stack([jnp.exp(-spread), 1.0 / norm]), ((0, 0), (1, LANES - NCLASS - 1)))


def exchange(low_edge, high_edge, axis):
    count = lax.axis_size(axis)
    forward = [(i, i + 1) for i in range(count - 1)]
    backward = [(target, source) for source, target in forward]
    return lax.ppermute(high_edge, axis, forward), lax.ppermute(low_edge, axis, backward)


def per_device(heights, sigma_class, window_class, sigma_table, window_table):
    tables = jnp.concatenate([class_tables(sigma_table), class_tables(window_table)], axis=0)
    tables = jnp.pad(tables, ((0, 4), (0, 0)))
    sigma_code = (sigma_class + 1).astype(jnp.bfloat16)
    window_code = (window_class + 1).astype(jnp.bfloat16)

    def row_edge(start, code_start):
        band_rows = heights[:, start:start + WIDE, :].reshape(BANDS * WIDE, COLS)
        return jnp.concatenate([band_rows, sigma_code[code_start:code_start + RADIUS]], axis=0)

    low, high = exchange(row_edge(0, 0), row_edge(ROWS - WIDE, ROWS - RADIUS), "lat")

    def column_edge(start, inner):
        cols = slice(start, start + WIDE)
        low_rows = low[:BANDS * WIDE, cols].reshape(BANDS, WIDE, WIDE)
        high_rows = high[:BANDS * WIDE, cols].reshape(BANDS, WIDE, WIDE)
        tall = jnp.concatenate([low_rows, heights[:, :, cols], high_rows], axis=1)
        tall = jnp.transpose(tall, (1, 0, 2)).reshape(FULL, BANDS * WIDE)
        code = jnp.concatenate([low[BANDS * WIDE:, cols], sigma_code[:, cols], high[BANDS * WIDE:, cols]], axis=0)
        near = jnp.pad(window_code[:, inner:inner + RADIUS].reshape(2, LANES, RADIUS), ((0, 0), (0, CODES - LANES), (0, 0)))
        pad = jnp.zeros((CODES, LANES - 3 * WIDE), jnp.bfloat16)
        packed = jnp.concatenate([code[:CODES], code[CODES:], near[0], near[1], pad], axis=1)
        return jnp.concatenate([tall, packed], axis=0)

    left, right = exchange(column_edge(0, 0), column_edge(COLS - WIDE, COLS - RADIUS), "lon")

    vmem = pl.BlockSpec(memory_space=pltpu.VMEM)
    return pl.pallas_call(
        kernel,
        out_shape=jax.ShapeDtypeStruct((BANDS, ROWS, COLS), jnp.bfloat16),
        in_specs=[vmem] * 8,
        out_specs=vmem,
        scratch_shapes=[
            pltpu.VMEM((18, FULL, LANES), jnp.float32),
            pltpu.VMEM((18, TALL, LANES), jnp.float32),
            pltpu.VMEM((9, COLS + 2 * WIDE, LANES), jnp.float32),
            pltpu.VMEM((9, BROAD, LANES), jnp.float32),
            pltpu.VMEM((6, TALL, LANES), jnp.int32),
            pltpu.VMEM((3, BROAD, LANES), jnp.int32),
            pltpu.VMEM((5, ROWS, LANES), jnp.int32),
            pltpu.VMEM((2, COLS, LANES), jnp.int32),
        ],
        name="smooth",
    )(tables, heights, low, high, left, right, sigma_class, window_class)


def solution(mesh):
    placed = (P(None, "lat", "lon"), P("lat", "lon"), P("lat", "lon"), P(), P())
    return jax.shard_map(
        per_device, mesh=mesh, in_specs=placed, out_specs=P(None, "lat", "lon"), check_vma=False
    )
```

```python
import jax
import jax.numpy as jnp
from jax import lax
from jax.experimental import pallas as pl
from jax.experimental.pallas import tpu as pltpu
from jax.sharding import PartitionSpec as P

RADIUS = 16
NCLASS = 16
BANDS = 4
ROWS = 256
COLS = 512
LANES = 128
COLBLK = COLS // LANES
ROWBLK = ROWS // LANES
WIDE = 2 * RADIUS
TALL = ROWS + 2 * RADIUS
FULL = ROWS + 2 * WIDE
BROAD = COLS + 2 * RADIUS
CODES = TALL // 2
UNROLL = 4


def lookup(table, codes):
    return jnp.take_along_axis(jnp.broadcast_to(table, codes.shape), codes, axis=1)


def weighted(sources, q, scale):
    square = q * q
    weight = q
    ratio = q * square
    totals = [source(0) for source in sources]
    for k in range(1, RADIUS + 1):
        if k > 1:
            weight = weight * ratio
            ratio = ratio * square
        totals = [
            total + weight * (source(k) + source(-k)) for total, source in zip(totals, sources)
        ]
    return [total * scale for total in totals]


def smooth_blocks(source_ref, blocks, lead, q_ref, s_ref, cell_block, out_ref, length, rounded=False):
    def tile(step, _):
        start = pl.multiple_of(step * 8, 8)
        q = q_ref[cell_block, pl.ds(start, 8), :]
        scale = s_ref[cell_block, pl.ds(start, 8), :]

        def reader(block):
            return lambda k: source_ref[block, pl.ds(start + lead + k, 8), :]

        results = weighted([reader(block) for block in blocks], q, scale)
        for block, result in zip(blocks, results):
            if rounded:
                result = result.astype(jnp.bfloat16).astype(jnp.float32)
            out_ref[block, pl.ds(start, 8), :] = result
        return 0

    lax.fori_loop(0, length // 8, tile, 0, unroll=UNROLL)


def kernel(
    tables_ref, heights_ref, low_ref, high_ref, left_ref, right_ref, sigma_ref, window_ref, out_ref,
    rows_in, rows_out, cols_in, cols_out, q_sig, s_sig, q_sig_t, s_sig_t, q_win, s_win, q_win_t, s_win_t,
):
    q_sig_tab = tables_ref[0:1, :]
    s_sig_tab = tables_ref[1:2, :]
    q_win_tab = tables_ref[2:3, :]
    s_win_tab = tables_ref[3:4, :]

    for b in range(BANDS):
        for j in range(COLBLK):
            lanes = slice(j * LANES, (j + 1) * LANES)
            block = b * COLBLK + j
            rows_in[block, 0:WIDE, :] = low_ref[b * WIDE:(b + 1) * WIDE, lanes].astype(jnp.float32)
            rows_in[block, WIDE:WIDE + ROWS, :] = heights_ref[b, :, lanes].astype(jnp.float32)
            rows_in[block, WIDE + ROWS:FULL, :] = high_ref[b * WIDE:(b + 1) * WIDE, lanes].astype(jnp.float32)
    rows_in[16, :, :] = left_ref[0:FULL, :].astype(jnp.float32)
    rows_in[17, :, :] = right_ref[0:FULL, :].astype(jnp.float32)

    def fill(q_ref, s_ref, block, rows, codes, q_tab, s_tab):
        codes = codes.astype(jnp.float32).astype(jnp.int32) if codes.dtype == jnp.bfloat16 else codes
        q_ref[block, rows, :] = lookup(q_tab, codes)
        s_ref[block, rows, :] = lookup(s_tab, codes)

    for j in range(COLBLK):
        lanes = slice(j * LANES, (j + 1) * LANES)
        edge = slice(BANDS * WIDE, BANDS * WIDE + RADIUS)
        fill(q_sig, s_sig, j, slice(0, RADIUS), low_ref[edge, lanes], q_sig_tab, s_sig_tab)
        fill(q_sig, s_sig, j, slice(RADIUS, RADIUS + ROWS), sigma_ref[:, lanes] + 1, q_sig_tab, s_sig_tab)
        fill(q_sig, s_sig, j, slice(RADIUS + ROWS, TALL), high_ref[edge, lanes], q_sig_tab, s_sig_tab)
        fill(q_win, s_win, j, slice(0, ROWS), window_ref[:, lanes] + 1, q_win_tab, s_win_tab)
    halves = []
    for side, ref in ((4, left_ref), (5, right_ref)):
        packed = ref[FULL:FULL + CODES, :].astype(jnp.float32).astype(jnp.int32)
        for half in range(2):
            piece = packed[:, half * WIDE:(half + 1) * WIDE]
            rows = slice(half * CODES, (half + 1) * CODES)
            fill(q_sig, s_sig, side, rows, jnp.concatenate([piece] * BANDS, axis=1), q_sig_tab, s_sig_tab)
        halves.append([packed[0:LANES, 2 * WIDE + h * RADIUS:2 * WIDE + (h + 1) * RADIUS] for h in range(2)])
    for half in range(2):
        pair = [halves[0][half], halves[1][half]]
        rows = slice(half * LANES, (half + 1) * LANES)
        fill(q_win, s_win, 4, rows, jnp.concatenate(pair * BANDS, axis=1), q_win_tab, s_win_tab)

    for sig_row, sig_col, win_row, win_col in ((q_sig, q_sig_t, q_win, q_win_t), (s_sig, s_sig_t, s_win, s_win_t)):
        for j in range(COLBLK):
            for i in range(ROWBLK):
                body = sig_row[j, RADIUS + i * LANES:RADIUS + (i + 1) * LANES, :]
                sig_col[i, RADIUS + j * LANES:RADIUS + (j + 1) * LANES, :] = body.T
                win_col[i, j * LANES:(j + 1) * LANES, :] = win_row[j, i * LANES:(i + 1) * LANES, :].T
            edges = jnp.concatenate([sig_row[j, 0:RADIUS, :], sig_row[j, RADIUS + ROWS:TALL, :]] * BANDS, axis=0)
            sig_col[2, RADIUS + j * LANES:RADIUS + (j + 1) * LANES, :] = edges.T
        for side, block in enumerate((4, 5)):
            inner = slice(RADIUS, WIDE) if side == 0 else slice(0, RADIUS)
            place = slice(0, RADIUS) if side == 0 else slice(RADIUS + COLS, BROAD)
            for i in range(ROWBLK):
                body = sig_row[block, RADIUS + i * LANES:RADIUS + (i + 1) * LANES, :].T
                sig_col[i, place, :] = body[inner, :]
            edges = jnp.concatenate([sig_row[block, 0:RADIUS, :], sig_row[block, RADIUS + ROWS:TALL, :]] * BANDS, axis=0)
            sig_col[2, place, :] = edges.T[inner, :]

    for j in range(COLBLK):
        blocks = [b * COLBLK + j for b in range(BANDS)]
        smooth_blocks(rows_in, blocks, RADIUS, q_sig, s_sig, j, rows_out, TALL)
    for side in range(2):
        smooth_blocks(rows_in, [16 + side], RADIUS, q_sig, s_sig, 4 + side, rows_out, TALL)

    for j in range(COLBLK):
        place = slice(WIDE + j * LANES, WIDE + (j + 1) * LANES)
        for b in range(BANDS):
            for i in range(ROWBLK):
                body = rows_out[b * COLBLK + j, RADIUS + i * LANES:RADIUS + (i + 1) * LANES, :]
                cols_in[b * ROWBLK + i, place, :] = body.T
        edges = []
        for b in range(BANDS):
            edges += [rows_out[b * COLBLK + j, 0:RADIUS, :], rows_out[b * COLBLK + j, RADIUS + ROWS:TALL, :]]
        cols_in[8, place, :] = jnp.concatenate(edges, axis=0).T
    for side in range(2):
        place = slice(0, WIDE) if side == 0 else slice(WIDE + COLS, 2 * WIDE + COLS)
        for i in range(ROWBLK):
            body = rows_out[16 + side, RADIUS + i * LANES:RADIUS + (i + 1) * LANES, :].T
            for b in range(BANDS):
                cols_in[b * ROWBLK + i, place, :] = body[b * WIDE:(b + 1) * WIDE, :]
        top = rows_out[16 + side, 0:RADIUS, :]
        bottom = rows_out[16 + side, RADIUS + ROWS:TALL, :]
        edges = jnp.concatenate([top, bottom] * BANDS, axis=0).T
        lane = lax.broadcasted_iota(jnp.int32, (WIDE, LANES), 1) // WIDE
        merged = edges[0:WIDE, :]
        for b in range(1, BANDS):
            merged = jnp.where(lane == b, edges[b * WIDE:(b + 1) * WIDE, :], merged)
        cols_in[8, place, :] = merged

    for i in range(ROWBLK):
        blocks = [b * ROWBLK + i for b in range(BANDS)]
        smooth_blocks(cols_in, blocks, RADIUS, q_sig_t, s_sig_t, i, cols_out, BROAD, True)
    smooth_blocks(cols_in, [8], RADIUS, q_sig_t, s_sig_t, 2, cols_out, BROAD, True)

    for j in range(COLBLK):
        place = slice(RADIUS + j * LANES, RADIUS + (j + 1) * LANES)
        for b in range(BANDS):
            for i in range(ROWBLK):
                rows_in[b * COLBLK + j, RADIUS + i * LANES:RADIUS + (i + 1) * LANES, :] = cols_out[b * ROWBLK + i, place, :].T
        edges = cols_out[8, place, :].T
        for b in range(BANDS):
            rows_in[b * COLBLK + j, 0:RADIUS, :] = edges[b * WIDE:b * WIDE + RADIUS, :]
            rows_in[b * COLBLK + j, RADIUS + ROWS:TALL, :] = edges[b * WIDE + RADIUS:(b + 1) * WIDE, :]
    for i in range(ROWBLK):
        edges = []
        for b in range(BANDS):
            edges += [cols_out[b * ROWBLK + i, 0:RADIUS, :], cols_out[b * ROWBLK + i, RADIUS + COLS:BROAD, :]]
        rows_in[16, RADIUS + i * LANES:RADIUS + (i + 1) * LANES, :] = jnp.concatenate(edges, axis=0).T
    both = jnp.concatenate([cols_out[8, 0:RADIUS, :], cols_out[8, RADIUS + COLS:BROAD, :]] * BANDS, axis=0).T
    lane = lax.broadcasted_iota(jnp.int32, (WIDE, LANES), 1) // WIDE
    merged = both[0:WIDE, :]
    for b in range(1, BANDS):
        merged = jnp.where(lane == b, both[b * WIDE:(b + 1) * WIDE, :], merged)
    rows_in[16, 0:RADIUS, :] = merged[0:RADIUS, :]
    rows_in[16, RADIUS + ROWS:TALL, :] = merged[RADIUS:WIDE, :]

    for j in range(COLBLK):
        blocks = [b * COLBLK + j for b in range(BANDS)]
        smooth_blocks(rows_in, blocks, RADIUS, q_win, s_win, j, rows_out, ROWS)
    smooth_blocks(rows_in, [16], RADIUS, q_win, s_win, 4, rows_out, ROWS)

    for i in range(ROWBLK):
        for j in range(COLBLK):
            for b in range(BANDS):
                body = rows_out[b * COLBLK + j, i * LANES:(i + 1) * LANES, :]
                cols_in[b * ROWBLK + i, RADIUS + j * LANES:RADIUS + (j + 1) * LANES, :] = body.T
        body = rows_out[16, i * LANES:(i + 1) * LANES, :].T
        for b in range(BANDS):
            cols_in[b * ROWBLK + i, 0:RADIUS, :] = body[b * WIDE:b * WIDE + RADIUS, :]
            cols_in[b * ROWBLK + i, RADIUS + COLS:BROAD, :] = body[b * WIDE + RADIUS:(b + 1) * WIDE, :]

    for i in range(ROWBLK):
        blocks = [b * ROWBLK + i for b in range(BANDS)]
        smooth_blocks(cols_in, blocks, RADIUS, q_win_t, s_win_t, i, cols_out, COLS)

    for b in range(BANDS):
        for i in range(ROWBLK):
            for j in range(COLBLK):
                body = cols_out[b * ROWBLK + i, j * LANES:(j + 1) * LANES, :].T
                out_ref[b, i * LANES:(i + 1) * LANES, j * LANES:(j + 1) * LANES] = body.astype(jnp.bfloat16)


def class_tables(table):
    spread = 0.5 / (table * table)
    offsets = jnp.arange(-RADIUS, RADIUS + 1).astype(jnp.float32)
    norm = jnp.sum(jnp.exp(-(offsets * offsets)[None, :] * spread[:, None]), axis=1)
    return jnp.pad(jnp.stack([jnp.exp(-spread), 1.0 / norm]), ((0, 0), (1, LANES - NCLASS - 1)))


def exchange(low_edge, high_edge, axis):
    count = lax.axis_size(axis)
    even = lax.axis_index(axis) % 2 == 0

    def swap(first):
        pairs = [(i, i + 1) for i in range(first, count - 1, 2)]
        return pairs + [(target, source) for source, target in pairs]

    near = lax.ppermute(jnp.where(even, high_edge, low_edge), axis, swap(0))
    far = lax.ppermute(jnp.where(even, low_edge, high_edge), axis, swap(1))
    return jnp.where(even, far, near), jnp.where(even, near, far)


def per_device(heights, sigma_class, window_class, sigma_table, window_table):
    tables = jnp.concatenate([class_tables(sigma_table), class_tables(window_table)], axis=0)
    tables = jnp.pad(tables, ((0, 4), (0, 0)))
    sigma_code = (sigma_class + 1).astype(jnp.bfloat16)
    window_code = (window_class + 1).astype(jnp.bfloat16)

    def row_edge(start, code_start):
        band_rows = heights[:, start:start + WIDE, :].reshape(BANDS * WIDE, COLS)
        return jnp.concatenate([band_rows, sigma_code[code_start:code_start + RADIUS]], axis=0)

    low, high = exchange(row_edge(0, 0), row_edge(ROWS - WIDE, ROWS - RADIUS), "lat")

    def column_edge(start, inner):
        cols = slice(start, start + WIDE)
        low_rows = low[:BANDS * WIDE, cols].reshape(BANDS, WIDE, WIDE)
        high_rows = high[:BANDS * WIDE, cols].reshape(BANDS, WIDE, WIDE)
        tall = jnp.concatenate([low_rows, heights[:, :, cols], high_rows], axis=1)
        tall = jnp.transpose(tall, (1, 0, 2)).reshape(FULL, BANDS * WIDE)
        code = jnp.concatenate([low[BANDS * WIDE:, cols], sigma_code[:, cols], high[BANDS * WIDE:, cols]], axis=0)
        near = jnp.pad(window_code[:, inner:inner + RADIUS].reshape(2, LANES, RADIUS), ((0, 0), (0, CODES - LANES), (0, 0)))
        pad = jnp.zeros((CODES, LANES - 3 * WIDE), jnp.bfloat16)
        packed = jnp.concatenate([code[:CODES], code[CODES:], near[0], near[1], pad], axis=1)
        return jnp.concatenate([tall, packed], axis=0)

    left, right = exchange(column_edge(0, 0), column_edge(COLS - WIDE, COLS - RADIUS), "lon")

    vmem = pl.BlockSpec(memory_space=pltpu.VMEM)
    return pl.pallas_call(
        kernel,
        out_shape=jax.ShapeDtypeStruct((BANDS, ROWS, COLS), jnp.bfloat16),
        in_specs=[vmem] * 8,
        out_specs=vmem,
        scratch_shapes=[
            pltpu.VMEM((18, FULL, LANES), jnp.float32),
            pltpu.VMEM((18, TALL, LANES), jnp.float32),
            pltpu.VMEM((9, COLS + 2 * WIDE, LANES), jnp.float32),
            pltpu.VMEM((9, BROAD, LANES), jnp.float32),
            pltpu.VMEM((6, TALL, LANES), jnp.float32),
            pltpu.VMEM((6, TALL, LANES), jnp.float32),
            pltpu.VMEM((3, BROAD, LANES), jnp.float32),
            pltpu.VMEM((3, BROAD, LANES), jnp.float32),
            pltpu.VMEM((5, ROWS, LANES), jnp.float32),
            pltpu.VMEM((5, ROWS, LANES), jnp.float32),
            pltpu.VMEM((2, COLS, LANES), jnp.float32),
            pltpu.VMEM((2, COLS, LANES), jnp.float32),
        ],
        name="smooth",
    )(tables, heights, low, high, left, right, sigma_class, window_class)


def solution(mesh):
    placed = (P(None, "lat", "lon"), P("lat", "lon"), P("lat", "lon"), P(), P())
    return jax.shard_map(
        per_device, mesh=mesh, in_specs=placed, out_specs=P(None, "lat", "lon"), check_vma=False
    )
```
